32 devices in a mesh: row: 8 (over z, x), rep: 4 (over y, core).
Axes of the slice: x: 2, y: 2, z: 4, core: 2. Of those that a mesh axis runs over, the one named last changes fastest.
Arguments:
- features: bfloat16 [16384, 4096], P('row'), may hold values from -6 to 6
- coefficients: bfloat16 [4096, 512], P('row', 'rep'), may hold values from -0.1875 to 0.1875
- multiplicity: int32 [16384, 512], P('row', 'rep'), may hold values from 0 to 3
- treated: int32 [16384], P('row'), may hold values from 0 to 1
- outcome: int32 [16384], P('row'), may hold values from 0 to 1
- offset: float32 [16384], P('row'), may hold values from -4 to 4
- trim_low: int32 [512], P('rep'), may hold values from -768 to -256
- trim_high: int32 [512], P('rep'), may hold values from 256 to 768
Outputs:
- new_coefficients: float32 [4096, 512], P('row', 'rep')
- score: float32 [4096, 512], P('row', 'rep')
- effect: float32 [2, 4, 128], P(None, 'rep', 'row')
The draws below stay inside these ranges and needn't reach their ends.
All inputs are finite; a program needn't handle non-finite values.
Results may differ from the reference program's by a relative error of at most 0.003.
Values may be sent and summed in bfloat16 or wider, within the bound.
A program may use at most 128 MiB of HBM per device.

```python
import jax
import jax.numpy as jnp
from jax import lax

P_SIZE = 4096
R = 512
ROWS_DEV = 2048
REFIT_ITERS = 2
N = 16384
N_REP = 4


def block_binary(key):
    blocks = N // ROWS_DEV
    key_rate, key_row = jax.random.split(key)
    rates = jax.random.randint(key_rate, (blocks,), 200, 801)
    level = jnp.repeat(rates, ROWS_DEV, total_repeat_length=N)
    draws = jax.random.randint(key_row, (N,), 0, 1000)
    return jnp.where(draws < level, 1, 0).astype(jnp.int32)


def draw_treated(key, part):
    return block_binary(jax.random.fold_in(key, 11))


def draw_outcome(key, part):
    return block_binary(jax.random.fold_in(key, 23))


def draw_offset(key, part):
    blocks = N // ROWS_DEV
    key_mean, key_row = jax.random.split(jax.random.fold_in(key, 37))
    centre = jax.random.uniform(key_mean, (blocks,), jnp.float32, -1.0, 1.0)
    ramp = 0.5 + 1.5 * jnp.arange(blocks).astype(jnp.float32) / max(blocks - 1, 1)
    level = jnp.repeat(centre * ramp, ROWS_DEV, total_repeat_length=N)
    noise = jnp.clip(0.5 * jax.random.normal(key_row, (N,), jnp.float32), -2.0, 2.0)
    return (level + noise).astype(jnp.float32)


def set_ends(result, stream_key, least, largest):
    index_at = [jax.random.randint(jax.random.fold_in(stream_key, axis), (), 0, length) for axis, length in enumerate(result.shape)]
    main_axis = result.shape.index(max(result.shape))
    next_to = index_at[:main_axis] + [(index_at[main_axis] + 1) % result.shape[main_axis]] + index_at[main_axis + 1:]
    return result.at[tuple(index_at)].set(least).at[tuple(next_to)].set(largest)


def level_of(stream_key, dims, shards, least, high):
    factor_of, own = 1.0, jax.random.fold_in(stream_key, 6)
    for position, parts in shards:
        steps = jnp.exp(jax.random.uniform(jax.random.fold_in(own, position), (parts,), jnp.float32, least / len(shards), high / len(shards)))
        factor_of = factor_of * jnp.repeat(steps, dims[position] // parts).reshape([-1 if axis == position else 1 for axis in range(len(dims))])
    return factor_of


def normal_values(own_key, extent, deviation, limit, cuts=(), held_as=jnp.bfloat16):
    values = jax.random.normal(own_key, extent, jnp.float32) * deviation
    if len(cuts) > 0:
        values = level_of(own_key, extent, cuts, -0.22, 0.18) * values
    return jnp.clip(values, min=-limit, max=limit).astype(held_as)


def setup_inputs(seed: int = 0) -> dict:
    keys = jax.random.split(jax.random.key(seed), 9)
    return {
        "features": normal_values(keys[0], (N, P_SIZE), 1.0, 6.0, ((0, 8),)),
        "coefficients": normal_values(keys[1], (P_SIZE, R), (2.0 / P_SIZE ** 0.5), 0.1875, ((0, 8), (1, 4))),
        "multiplicity": set_ends(jax.random.randint(keys[2], (N, R), 0, 4), jax.random.fold_in(keys[2], 1), 0, 3).astype(jnp.int32),
        "treated": draw_treated(jax.random.fold_in(keys[8], 71), 0),
        "outcome": draw_outcome(jax.random.fold_in(keys[8], 71), 0),
        "offset": draw_offset(jax.random.fold_in(keys[8], 71), 0),
        "trim_low": set_ends(jax.random.randint(keys[6], (R,), -768, -255), jax.random.fold_in(keys[6], 1), -768, (-255) - 1).astype(jnp.int32),
        "trim_high": set_ends(jax.random.randint(keys[7], (R,), 256, 769), jax.random.fold_in(keys[7], 1), 256, 768).astype(jnp.int32),
    }


def refit_update(a_coef, c_coef, ipw, treat, target, offset):
    prob = jax.nn.sigmoid(a_coef[None, :] + c_coef[None, :] * treat[:, None] + offset[:, None])
    res = ipw * (target[:, None] - prob)
    cur = ipw * prob * (1.0 - prob)
    ga = lax.optimization_barrier(jnp.sum(res, axis=0))
    gc = lax.optimization_barrier(jnp.sum(res * treat[:, None], axis=0))
    s_all = lax.optimization_barrier(jnp.sum(cur, axis=0))
    s_tr = lax.optimization_barrier(jnp.sum(cur * treat[:, None], axis=0))
    h11 = s_all + 1.0
    h22 = s_tr + 1.0
    det = h11 * h22 - s_tr * s_tr
    return (a_coef + (h22 * ga - s_tr * gc) / det, c_coef + (h11 * gc - s_tr * ga) / det)

def reference(features, coefficients, multiplicity, treated, outcome, offset, trim_low, trim_high):
    logits = jnp.dot(features, coefficients, preferred_element_type=jnp.float32)
    low = trim_low.astype(jnp.float32) / 256.0
    high = trim_high.astype(jnp.float32) / 256.0
    prop = jax.nn.sigmoid(jnp.minimum(jnp.maximum(logits, low[None, :]), high[None, :]))
    weight = multiplicity.astype(jnp.float32)
    treat = treated.astype(jnp.float32)
    target = outcome.astype(jnp.float32)
    resid = (weight * (treat[:, None] - prop)).astype(jnp.bfloat16)
    curv = (weight * prop * (1.0 - prop)).astype(jnp.bfloat16)
    squared = (features.astype(jnp.float32) * features.astype(jnp.float32)).astype(jnp.bfloat16)
    grad = jnp.dot(features.T, resid, preferred_element_type=jnp.float32)
    hess = jnp.dot(squared.T, curv, preferred_element_type=jnp.float32)
    new_coefficients = coefficients.astype(jnp.float32) + grad / (hess + 1.0)
    score = grad / jnp.sqrt(hess + 1.0)
    ipw = weight * (treat[:, None] / prop + (1.0 - treat[:, None]) / (1.0 - prop))
    a_coef = jnp.zeros((R,), jnp.float32)
    c_coef = jnp.zeros((R,), jnp.float32)
    for step in range(REFIT_ITERS):
        a_coef, c_coef = refit_update(a_coef, c_coef, ipw, treat, target, offset)
    effect = jnp.stack([a_coef, c_coef]).reshape(2, N_REP, R // N_REP)
    return (new_coefficients, score, effect)
```

```python
import functools

import jax
import jax.numpy as jnp
from jax import lax
from jax.experimental import pallas as pl
from jax.experimental.pallas import tpu as pltpu
from jax.sharding import PartitionSpec as P

REFIT_ITERS = 2
TILE = 128
F32 = jnp.float32
BF16 = jnp.bfloat16


def newton_step(a_coef, c_coef, stats):
    ga = stats[0:1]
    gc = stats[1:2]
    s_all = stats[2:3]
    s_tr = stats[3:4]
    h11 = s_all + 1.0
    h22 = s_tr + 1.0
    det = h11 * h22 - s_tr * s_tr
    return (a_coef + (h22 * ga - s_tr * gc) / det, c_coef + (h11 * gc - s_tr * ga) / det)


def kernel(
    n,
    feat_hbm,
    mult_hbm,
    coef_ref,
    side_ref,
    bounds_ref,
    new_ref,
    score_ref,
    eff_ref,
    feat,
    mult,
    coef_all,
    acc,
    ipw,
    resid,
    curv,
    keep,
    xsend,
    xrecv,
    zsend,
    zrecv,
    sums,
    stat_send,
    stat_recv,
    feat_sem,
    mult_sem,
    ag_send,
    ag_fwd,
    ag_recv,
    x_send,
    x_recv,
    z_send,
    z_recv,
    st_send,
    st_recv,
):
    outer = n // 2
    rep, width = acc.shape
    cols = coef_ref.shape[0]
    tiles = width // TILE
    me = lax.axis_index("row")
    mo = me // 2
    mx = lax.rem(me, 2)
    px = 1 - mx
    partner = 2 * mo + px

    def block(o, x):
        return 2 * o + x

    def shifted(i):
        return lax.rem(mo + i, outer)

    def behind(i):
        return lax.rem(mo - i + outer, outer)

    def remote(src, dst, send, recv, row):
        return pltpu.make_async_remote_copy(
            src_ref=src,
            dst_ref=dst,
            send_sem=send,
            recv_sem=recv,
            device_id={"row": row},
            device_id_type=pl.DeviceIdType.MESH,
        )

    def feat_copy(b):
        start = pl.multiple_of(b * cols, cols)
        return pltpu.make_async_copy(feat_hbm.at[:, pl.ds(start, cols)], feat.at[b], feat_sem.at[b])

    @pl.loop(0, outer)
    def _(i):
        o = behind(i)
        feat_copy(block(o, mx)).start()
        feat_copy(block(o, px)).start()

    mult_copy = pltpu.make_async_copy(mult_hbm, mult, mult_sem)
    mult_copy.start()

    barrier = pltpu.get_barrier_semaphore()
    for j in range(1, n):
        pl.semaphore_signal(
            barrier,
            inc=1,
            device_id={"row": lax.rem(me + j, n)},
            device_id_type=pl.DeviceIdType.MESH,
        )
    coef_all[me] = coef_ref[...].astype(F32).T.astype(BF16)
    pl.semaphore_wait(barrier, n - 1)

    def outer_copy(i):
        return remote(coef_all.at[me], coef_all.at[me], ag_send.at[i], ag_recv.at[me], block(shifted(i), mx))

    def forward_copy(o):
        b = block(o, mx)
        return remote(coef_all.at[b], coef_all.at[b], ag_fwd.at[o], ag_recv.at[b], partner)

    def coef_wait(b):
        remote(coef_all.at[b], coef_all.at[b], ag_fwd.at[0], ag_recv.at[b], partner).wait_recv()

    forward_copy(mo).start()

    @pl.loop(1, outer)
    def _(i):
        outer_copy(i).start()

    def logits_of(b, first):
        feat_copy(b).wait()
        part = lax.dot_general(
            coef_all[b], feat[b], (((1,), (1,)), ((), ())), preferred_element_type=F32
        )
        if first:
            acc[...] = part
        else:
            acc[...] += part

    logits_of(me, True)

    @pl.loop(1, outer)
    def _(i):
        o = behind(i)
        b = block(o, mx)
        coef_wait(b)
        forward_copy(o).start()
        logits_of(b, False)
        q = block(behind(i - 1), px)
        coef_wait(q)
        logits_of(q, False)

    last = block(behind(outer - 1), px)
    coef_wait(last)
    logits_of(last, False)

    low = jnp.broadcast_to(bounds_ref[0:1, :], (TILE, rep)).T
    high = jnp.broadcast_to(bounds_ref[1:2, :], (TILE, rep)).T
    mult_copy.wait()

    def add_sums(weighted, prob, treat, target):
        res = weighted * (target - prob)
        cur = weighted * (prob * (1.0 - prob))
        sums[0] += res
        sums[1] += res * treat
        sums[2] += cur
        sums[3] += cur * treat

    sums[...] = jnp.zeros_like(sums)

    @pl.loop(0, tiles)
    def _(t):
        start = pl.multiple_of(t * TILE, TILE)
        at = pl.ds(start, TILE)
        logit = jnp.minimum(jnp.maximum(acc[:, at], low), high)
        prop = 1.0 / (1.0 + jnp.exp(-logit))
        weight = mult[at, :].astype(F32).T
        treat = side_ref[0:1, at]
        target = side_ref[1:2, at]
        offset = side_ref[2:3, at]
        resid[:, at] = (weight * (treat - prop)).astype(BF16)
        curv[:, at] = (weight * prop * (1.0 - prop)).astype(BF16)
        weighted = weight * (1.0 + jnp.exp(jnp.where(treat > 0.5, -logit, logit)))
        ipw[:, at] = weighted
        add_sums(weighted, 1.0 / (1.0 + jnp.exp(-offset)), treat, target)

    def stat_copy(it, j):
        to = lax.rem(me + j, n)
        return remote(stat_send.at[it], stat_recv.at[it, me], st_send.at[it, j], st_recv.at[it, me], to)

    def send_stats(it):
        for k in range(4):
            stat_send[it, k : k + 1, :] = jnp.sum(sums[k].T, axis=0, keepdims=True)
        stat_send[it, 4:8, :] = jnp.zeros((4, rep), F32)
        stat_recv[it, me] = stat_send[it]
        @pl.loop(1, n)
        def _(j):
            stat_copy(it, j).start()

    def total_stats(it):
        @pl.loop(1, n)
        def _(j):
            src = lax.rem(me + j, n)
            remote(stat_send.at[it], stat_recv.at[it, src], st_send.at[it, j], st_recv.at[it, src], src).wait_recv()
            stat_copy(it, j).wait_send()

        return jnp.sum(stat_recv[it], axis=0)

    send_stats(0)

    def x_copy(o, k):
        return remote(xsend.at[o, k], xrecv.at[o, k], x_send.at[o, k], x_recv.at[o, k], partner)

    def z_copy(o, k):
        return remote(zsend.at[o, k], zrecv.at[mo, k], z_send.at[o, k], z_recv.at[mo, k], block(o, mx))

    def products(b, k):
        if k == 0:
            return jnp.dot(resid[...], feat[b], preferred_element_type=F32)
        wide = feat[b].astype(F32)
        return jnp.dot(curv[...], (wide * wide).astype(BF16), preferred_element_type=F32)

    def compute(o):
        for k in range(2):
            xsend[o, k] = products(block(o, px), k).astype(BF16)
            x_copy(o, k).start()
        for k in range(2):
            keep[o, k] = products(block(o, mx), k)

    def pass_on(o):
        for k in range(2):
            x_copy(o, k).wait_recv()
            zsend[o, k] = (keep[o, k] + xrecv[o, k].astype(F32)).astype(BF16)
            z_copy(o, k).start()

    compute(shifted(1))

    @pl.loop(2, outer + 1)
    def _(i):
        compute(shifted(i))
        pass_on(shifted(i - 1))

    zero = jnp.zeros((1, rep), F32)
    a_row, c_row = newton_step(zero, zero, total_stats(0))
    a_wide = jnp.broadcast_to(a_row, (TILE, rep)).T
    c_wide = jnp.broadcast_to(c_row, (TILE, rep)).T
    sums[...] = jnp.zeros_like(sums)

    @pl.loop(0, tiles)
    def _(t):
        start = pl.multiple_of(t * TILE, TILE)
        at = pl.ds(start, TILE)
        treat = side_ref[0:1, at]
        target = side_ref[1:2, at]
        offset = side_ref[2:3, at]
        prob = 1.0 / (1.0 + jnp.exp(-(a_wide + c_wide * treat + offset)))
        add_sums(ipw[:, at], prob, treat, target)

    send_stats(1)

    for k in range(2):
        x_copy(mo, k).wait_recv()
        keep[mo, k] = keep[mo, k] + xrecv[mo, k].astype(F32)

    @pl.loop(1, outer)
    def _(i):
        o = behind(i)
        for k in range(2):
            remote(zsend.at[o, k], zrecv.at[o, k], z_send.at[o, k], z_recv.at[o, k], block(o, mx)).wait_recv()
            keep[mo, k] = keep[mo, k] + zrecv[o, k].astype(F32)

    grad = keep[mo, 0].T
    hess = keep[mo, 1].T + 1.0
    new_ref[...] = coef_ref[...].astype(F32) + grad / hess
    score_ref[...] = grad / jnp.sqrt(hess)

    a_row, c_row = newton_step(a_row, c_row, total_stats(1))
    eff_ref[0:1, :] = a_row
    eff_ref[1:2, :] = c_row

    @pl.loop(0, outer)
    def _(o):
        forward_copy(o).wait_send()
        for k in range(2):
            x_copy(o, k).wait_send()

    @pl.loop(1, outer)
    def _(i):
        outer_copy(i).wait_send()
        for k in range(2):
            z_copy(shifted(i), k).wait_send()


def local(n, features, coefficients, multiplicity, treated, outcome, offset, trim_low, trim_high):
    rows, depth = features.shape
    cols, rep = coefficients.shape
    outer = n // 2
    side = jnp.stack([treated.astype(F32), outcome.astype(F32), offset])
    bounds = jnp.stack([trim_low, trim_high]).astype(F32) / 256.0
    anywhere = pl.BlockSpec(memory_space=pl.ANY)
    vmem = pl.BlockSpec(memory_space=pltpu.VMEM)
    dma = pltpu.SemaphoreType.DMA
    new_coefficients, score, eff = pl.pallas_call(
        functools.partial(kernel, n),
        out_shape=(
            jax.ShapeDtypeStruct((cols, rep), F32),
            jax.ShapeDtypeStruct((cols, rep), F32),
            jax.ShapeDtypeStruct((2, rep), F32),
        ),
        in_specs=[anywhere, anywhere, vmem, vmem, vmem],
        out_specs=(vmem, vmem, vmem),
        scratch_shapes=[
            pltpu.VMEM((n, rows, cols), BF16),
            pltpu.VMEM((rows, rep), jnp.int32),
            pltpu.VMEM((n, rep, cols), BF16),
            pltpu.VMEM((rep, rows), F32),
            pltpu.VMEM((rep, rows), F32),
            pltpu.VMEM((rep, rows), BF16),
            pltpu.VMEM((rep, rows), BF16),
            pltpu.VMEM((outer, 2, rep, cols), F32),
            pltpu.VMEM((outer, 2, rep, cols), BF16),
            pltpu.VMEM((outer, 2, rep, cols), BF16),
            pltpu.VMEM((outer, 2, rep, cols), BF16),
            pltpu.VMEM((outer, 2, rep, cols), BF16),
            pltpu.VMEM((4, rep, TILE), F32),
            pltpu.VMEM((REFIT_ITERS, 8, rep), F32),
            pltpu.VMEM((REFIT_ITERS, n, 8, rep), F32),
            dma((n,)),
            dma(()),
            dma((outer,)),
            dma((outer,)),
            dma((n,)),
            dma((outer, 2)),
            dma((outer, 2)),
            dma((outer, 2)),
            dma((outer, 2)),
            dma((REFIT_ITERS, n)),
            dma((REFIT_ITERS, n)),
        ],
        compiler_params=pltpu.CompilerParams(
            collective_id=0, has_side_effects=True, vmem_limit_bytes=52 * 1024 * 1024
        ),
        name="propensity",
    )(features, multiplicity, coefficients, side, bounds)
    owned = rep // n
    mine = lax.dynamic_slice_in_dim(eff, lax.axis_index("row") * owned, owned, axis=1)
    return (new_coefficients, score, mine.reshape(2, 1, owned))


def solution(mesh):
    return jax.shard_map(
        functools.partial(local, mesh.shape["row"]),
        mesh=mesh,
        in_specs=(
            P("row", None),
            P("row", "rep"),
            P("row", "rep"),
            P("row"),
            P("row"),
            P("row"),
            P("rep"),
            P("rep"),
        ),
        out_specs=(P("row", "rep"), P("row", "rep"), P(None, "rep", "row")),
        check_vma=False,
    )
```

```python
import functools

import jax
import jax.numpy as jnp
from jax import lax
from jax.experimental import pallas as pl
from jax.experimental.pallas import tpu as pltpu
from jax.sharding import PartitionSpec as P

REFIT_ITERS = 2
TILE = 128
F32 = jnp.float32
BF16 = jnp.bfloat16


def newton_step(a_coef, c_coef, stats):
    ga = stats[0:1]
    gc = stats[1:2]
    s_all = stats[2:3]
    s_tr = stats[3:4]
    h11 = s_all + 1.0
    h22 = s_tr + 1.0
    det = h11 * h22 - s_tr * s_tr
    return (a_coef + (h22 * ga - s_tr * gc) / det, c_coef + (h11 * gc - s_tr * ga) / det)


def kernel(
    n,
    feat_hbm,
    mult_hbm,
    coef_hbm,
    treat_hbm,
    target_hbm,
    offset_hbm,
    low_hbm,
    high_hbm,
    grad_ref,
    hess_ref,
    eff_ref,
    feat,
    mult,
    coef,
    treat_ref,
    target_ref,
    offset_ref,
    low_ref,
    high_ref,
    coef_all,
    wide_weight,
    acc,
    ipw,
    resid,
    curv,
    keep,
    xsend,
    xrecv,
    zsend,
    zrecv,
    sums,
    stat_send,
    stat_recv,
    feat_sem,
    mult_sem,
    coef_sem,
    side_sem,
    ag_up,
    ag_down,
    ag_fwd,
    ag_recv,
    x_send,
    x_recv,
    z_send,
    z_recv,
    st_send,
    st_recv,
):
    outer = n // 2
    rep, width = acc.shape
    cols = coef.shape[0]
    tiles = width // TILE
    me = lax.axis_index("row")
    mo = me // 2
    mx = lax.rem(me, 2)
    px = 1 - mx
    partner = 2 * mo + px

    def block(o, x):
        return 2 * o + x

    low_side = 1 - (2 * mo) // outer
    near = low_side * mo + (1 - low_side) * (outer - 1 - mo)
    far = outer - 1 - near

    def target_of(i):
        j = i - (far - near)
        both = mo + (1 - 2 * lax.rem(j + 2 * outer, 2)) * (near - (j + 2 * outer) // 2 + outer)
        return jnp.where(j < 0, mo + (2 * low_side - 1) * (far - i), both)

    def remote(src, dst, send, recv, row):
        return pltpu.make_async_remote_copy(
            src_ref=src,
            dst_ref=dst,
            send_sem=send,
            recv_sem=recv,
            device_id={"row": row},
            device_id_type=pl.DeviceIdType.MESH,
        )

    def feat_copy(b):
        start = pl.multiple_of(b * cols, cols)
        return pltpu.make_async_copy(feat_hbm.at[:, pl.ds(start, cols)], feat.at[b], feat_sem.at[b])

    coef_copy = pltpu.make_async_copy(coef_hbm, coef, coef_sem)
    coef_copy.start()
    mult_copy = pltpu.make_async_copy(mult_hbm, mult, mult_sem)
    mult_copy.start()
    pairs = (
        (treat_hbm, treat_ref),
        (target_hbm, target_ref),
        (offset_hbm, offset_ref),
        (low_hbm, low_ref),
        (high_hbm, high_ref),
    )
    side_copies = [pltpu.make_async_copy(a, b, side_sem.at[i]) for i, (a, b) in enumerate(pairs)]
    for copy in side_copies:
        copy.start()

    barrier = pltpu.get_barrier_semaphore()
    for j in range(1, n):
        pl.semaphore_signal(
            barrier,
            inc=1,
            device_id={"row": lax.rem(me + j, n)},
            device_id_type=pl.DeviceIdType.MESH,
        )
    coef_copy.wait()
    coef_all[me] = coef[...].astype(F32).T.astype(BF16)
    pl.semaphore_wait(barrier, n - 1)

    def up_copy(o):
        b = block(o, mx)
        return remote(coef_all.at[b], coef_all.at[b], ag_up.at[o], ag_recv.at[b], block(mo + 1, mx))

    def down_copy(o):
        b = block(o, mx)
        return remote(coef_all.at[b], coef_all.at[b], ag_down.at[o], ag_recv.at[b], block(mo - 1, mx))

    def forward_copy(o):
        b = block(o, mx)
        return remote(coef_all.at[b], coef_all.at[b], ag_fwd.at[o], ag_recv.at[b], partner)

    def coef_wait(b):
        remote(coef_all.at[b], coef_all.at[b], ag_fwd.at[0], ag_recv.at[b], partner).wait_recv()

    has_up = mo + 1 < outer
    has_down = mo > 0

    @pl.when(has_up)
    def _():
        up_copy(mo).start()

    @pl.when(has_down)
    def _():
        down_copy(mo).start()

    forward_copy(mo).start()

    feat_copy(me).start()
    feat_copy(partner).start()

    @pl.loop(1, outer)
    def _(i):
        @pl.when(mo - i >= 0)
        def _():
            feat_copy(block(mo - i, mx)).start()
            feat_copy(block(mo - i, px)).start()

        @pl.when(mo + i < outer)
        def _():
            feat_copy(block(mo + i, mx)).start()
            feat_copy(block(mo + i, px)).start()

    mult_copy.wait()
    for copy in side_copies:
        copy.wait()

    @pl.loop(0, tiles)
    def _(t):
        at = pl.ds(pl.multiple_of(t * TILE, TILE), TILE)
        wide_weight[:, at] = mult[at, :].astype(F32).T

    def logits_of(b, first):
        feat_copy(b).wait()
        part = lax.dot_general(
            coef_all[b], feat[b], (((1,), (1,)), ((), ())), preferred_element_type=F32
        )
        if first:
            acc[...] = part
        else:
            acc[...] += part

    logits_of(me, True)

    def arrived(b):
        coef_wait(b)
        logits_of(b, False)

    @pl.loop(1, outer)
    def _(i):
        below = mo - i
        above = mo + i

        @pl.when(below >= 0)
        def _():
            coef_wait(block(below, mx))

            @pl.when(has_up)
            def _():
                up_copy(below).start()

            forward_copy(below).start()

        @pl.when(above < outer)
        def _():
            coef_wait(block(above, mx))

            @pl.when(has_down)
            def _():
                down_copy(above).start()

            forward_copy(above).start()

        @pl.when(below >= 0)
        def _():
            logits_of(block(below, mx), False)

        @pl.when(above < outer)
        def _():
            logits_of(block(above, mx), False)

        @pl.when(below + 1 >= 0)
        def _():
            arrived(block(below + 1, px))

        @pl.when(jnp.logical_and(above - 1 < outer, i > 1))
        def _():
            arrived(block(above - 1, px))

    @pl.when(mo == outer - 1)
    def _():
        arrived(block(0, px))

    @pl.when(mo == 0)
    def _():
        arrived(block(outer - 1, px))

    low = jnp.broadcast_to(low_ref[...].astype(F32) / 256.0, (TILE, rep)).T
    high = jnp.broadcast_to(high_ref[...].astype(F32) / 256.0, (TILE, rep)).T

    def add_sums(weighted, prob, treat, target):
        res = weighted * (target - prob)
        cur = weighted * (prob * (1.0 - prob))
        sums[0] += res
        sums[1] += res * treat
        sums[2] += cur
        sums[3] += cur * treat

    @pl.loop(0, tiles)
    def _(t):
        at = pl.ds(pl.multiple_of(t * TILE, TILE), TILE)
        logit = jnp.minimum(jnp.maximum(acc[:, at], low), high)
        prop = 1.0 / (1.0 + jnp.exp(-logit))
        weight = wide_weight[:, at]
        treat = treat_ref[:, at].astype(F32)
        resid[:, at] = (weight * (treat - prop)).astype(BF16)
        curv[:, at] = (weight * prop * (1.0 - prop)).astype(BF16)

    def first_sums():
        sums[...] = jnp.zeros_like(sums)

        @pl.loop(0, tiles)
        def _(t):
            at = pl.ds(pl.multiple_of(t * TILE, TILE), TILE)
            logit = jnp.minimum(jnp.maximum(acc[:, at], low), high)
            treat = treat_ref[:, at].astype(F32)
            target = target_ref[:, at].astype(F32)
            weighted = wide_weight[:, at] * (1.0 + jnp.exp(jnp.where(treat > 0.5, -logit, logit)))
            ipw[:, at] = weighted
            add_sums(weighted, 1.0 / (1.0 + jnp.exp(-offset_ref[:, at])), treat, target)

    def stat_copy(it, j):
        to = lax.rem(me + j, n)
        return remote(stat_send.at[it], stat_recv.at[it, me], st_send.at[it, j], st_recv.at[it, me], to)

    def send_stats(it):
        for k in range(4):
            stat_send[it, k : k + 1, :] = jnp.sum(sums[k].T, axis=0, keepdims=True)
        stat_send[it, 4:8, :] = jnp.zeros((4, rep), F32)
        stat_recv[it, me] = stat_send[it]
        @pl.loop(1, n)
        def _(j):
            stat_copy(it, j).start()

    def total_stats(it):
        @pl.loop(1, n)
        def _(j):
            src = lax.rem(me + j, n)
            remote(stat_send.at[it], stat_recv.at[it, src], st_send.at[it, j], st_recv.at[it, src], src).wait_recv()
            stat_copy(it, j).wait_send()

        return jnp.sum(stat_recv[it], axis=0)

    def x_copy(o, k):
        return remote(xsend.at[o, k], xrecv.at[o, k], x_send.at[o, k], x_recv.at[o, k], partner)

    def z_up(o, k):
        return remote(zsend.at[o, k], zrecv.at[o, k], z_send.at[o, k], z_recv.at[o, k], block(mo + 1, mx))

    def z_down(o, k):
        slot = jnp.where(o == mo - 1, outer, o)
        return remote(zsend.at[o, k], zrecv.at[slot, k], z_send.at[o, k], z_recv.at[slot, k], block(mo - 1, mx))

    def z_wait(slot, k):
        remote(zsend.at[0, k], zrecv.at[slot, k], z_send.at[0, k], z_recv.at[slot, k], partner).wait_recv()

    def products(b, k):
        if k == 0:
            return jnp.dot(resid[...], feat[b], preferred_element_type=F32)
        wide = feat[b].astype(F32)
        return jnp.dot(curv[...], (wide * wide).astype(BF16), preferred_element_type=F32)

    def compute(o):
        for k in range(2):
            xsend[o, k] = products(block(o, px), k).astype(BF16)
            x_copy(o, k).start()
        for k in range(2):
            keep[o, k] = products(block(o, mx), k)

    def add_in(o, slot, k):
        z_wait(slot, k)
        keep[o, k] += zrecv[slot, k].astype(F32)

    def pass_on(o):
        for k in range(2):
            x_copy(o, k).wait_recv()
            keep[o, k] += xrecv[o, k].astype(F32)

            @pl.when(jnp.logical_or(jnp.logical_and(o > mo, has_down), jnp.logical_and(o < mo, has_up)))
            def _():
                add_in(o, o, k)

            zsend[o, k] = keep[o, k].astype(BF16)

            @pl.when(o > mo)
            def _():
                z_up(o, k).start()

            @pl.when(o < mo)
            def _():
                z_down(o, k).start()

    compute(target_of(0))
    first_sums()
    send_stats(0)
    compute(target_of(1))

    @pl.loop(2, outer)
    def _(i):
        compute(target_of(i))

        @pl.when(i < outer - 1)
        def _():
            pass_on(target_of(i - 2))

    zero = jnp.zeros((1, rep), F32)
    a_row, c_row = newton_step(zero, zero, total_stats(0))
    a_wide = jnp.broadcast_to(a_row, (TILE, rep)).T
    c_wide = jnp.broadcast_to(c_row, (TILE, rep)).T
    sums[...] = jnp.zeros_like(sums)

    @pl.loop(0, tiles)
    def _(t):
        at = pl.ds(pl.multiple_of(t * TILE, TILE), TILE)
        treat = treat_ref[:, at].astype(F32)
        target = target_ref[:, at].astype(F32)
        offset = offset_ref[:, at]
        prob = 1.0 / (1.0 + jnp.exp(-(a_wide + c_wide * treat + offset)))
        add_sums(ipw[:, at], prob, treat, target)

    send_stats(1)

    for i in range(max(outer - 3, 0), outer - 1):
        pass_on(target_of(i))

    for k in range(2):
        x_copy(mo, k).wait_recv()
        keep[mo, k] += xrecv[mo, k].astype(F32)

        @pl.when(has_down)
        def _():
            add_in(mo, mo, k)

        @pl.when(has_up)
        def _():
            add_in(mo, outer, k)

    grad_ref[...] = keep[mo, 0].T
    hess_ref[...] = keep[mo, 1].T

    a_row, c_row = newton_step(a_row, c_row, total_stats(1))
    eff_ref[0:1, :] = a_row
    eff_ref[1:2, :] = c_row

    @pl.loop(0, outer)
    def _(o):
        forward_copy(o).wait_send()
        for k in range(2):
            x_copy(o, k).wait_send()

        @pl.when(has_up)
        def _():
            @pl.when(o <= mo)
            def _():
                up_copy(o).wait_send()

            @pl.when(o > mo)
            def _():
                for k in range(2):
                    z_up(o, k).wait_send()

        @pl.when(has_down)
        def _():
            @pl.when(o >= mo)
            def _():
                down_copy(o).wait_send()

            @pl.when(o < mo)
            def _():
                for k in range(2):
                    z_down(o, k).wait_send()


def local(n, features, coefficients, multiplicity, treated, outcome, offset, trim_low, trim_high):
    rows, depth = features.shape
    cols, rep = coefficients.shape
    outer = n // 2
    hbm = pl.BlockSpec(memory_space=pltpu.HBM)
    vmem = pl.BlockSpec(memory_space=pltpu.VMEM)
    dma = pltpu.SemaphoreType.DMA
    grad, hess, eff = pl.pallas_call(
        functools.partial(kernel, n),
        out_shape=(
            jax.ShapeDtypeStruct((cols, rep), F32),
            jax.ShapeDtypeStruct((cols, rep), F32),
            jax.ShapeDtypeStruct((2, rep), F32),
        ),
        in_specs=[hbm] * 8,
        out_specs=(vmem, vmem, vmem),
        scratch_shapes=[
            pltpu.VMEM((n, rows, cols), BF16),
            pltpu.VMEM((rows, rep), jnp.int32),
            pltpu.VMEM((cols, rep), BF16),
            pltpu.VMEM((1, rows), jnp.int32),
            pltpu.VMEM((1, rows), jnp.int32),
            pltpu.VMEM((1, rows), F32),
            pltpu.VMEM((1, rep), jnp.int32),
            pltpu.VMEM((1, rep), jnp.int32),
            pltpu.VMEM((n, rep, cols), BF16),
            pltpu.VMEM((rep, rows), F32),
            pltpu.VMEM((rep, rows), F32),
            pltpu.VMEM((rep, rows), F32),
            pltpu.VMEM((rep, rows), BF16),
            pltpu.VMEM((rep, rows), BF16),
            pltpu.VMEM((outer, 2, rep, cols), F32),
            pltpu.VMEM((outer, 2, rep, cols), BF16),
            pltpu.VMEM((outer, 2, rep, cols), BF16),
            pltpu.VMEM((outer, 2, rep, cols), BF16),
            pltpu.VMEM((outer + 1, 2, rep, cols), BF16),
            pltpu.VMEM((4, rep, TILE), F32),
            pltpu.VMEM((REFIT_ITERS, 8, rep), F32),
            pltpu.VMEM((REFIT_ITERS, n, 8, rep), F32),
            dma((n,)),
            dma(()),
            dma(()),
            dma((5,)),
            dma((outer,)),
            dma((outer,)),
            dma((outer,)),
            dma((n,)),
            dma((outer, 2)),
            dma((outer, 2)),
            dma((outer, 2)),
            dma((outer + 1, 2)),
            dma((REFIT_ITERS, n)),
            dma((REFIT_ITERS, n)),
        ],
        compiler_params=pltpu.CompilerParams(
            collective_id=0, has_side_effects=True, vmem_limit_bytes=63 * 1024 * 1024
        ),
        name="propensity",
    )(
        features,
        multiplicity,
        coefficients,
        treated.reshape(1, rows),
        outcome.reshape(1, rows),
        offset.reshape(1, rows),
        trim_low.reshape(1, rep),
        trim_high.reshape(1, rep),
    )
    hess = hess + 1.0
    new_coefficients = coefficients.astype(F32) + grad / hess
    score = grad / jnp.sqrt(hess)
    owned = rep // n
    mine = lax.dynamic_slice_in_dim(eff, lax.axis_index("row") * owned, owned, axis=1)
    return (new_coefficients, score, mine.reshape(2, 1, owned))


def solution(mesh):
    return jax.shard_map(
        functools.partial(local, mesh.shape["row"]),
        mesh=mesh,
        in_specs=(
            P("row", None),
            P("row", "rep"),
            P("row", "rep"),
            P("row"),
            P("row"),
            P("row"),
            P("rep"),
            P("rep"),
        ),
        out_specs=(P("row", "rep"), P("row", "rep"), P(None, "rep", "row")),
        check_vma=False,
    )
```

```python
import functools

import jax
import jax.numpy as jnp
from jax import lax
from jax.experimental import pallas as pl
from jax.experimental.pallas import tpu as pltpu
from jax.sharding import PartitionSpec as P

REFIT_ITERS = 2
TILE = 128
PIECES = 2
F32 = jnp.float32
BF16 = jnp.bfloat16


def newton_step(a_coef, c_coef, stats):
    ga = stats[0:1]
    gc = stats[1:2]
    s_all = stats[2:3]
    s_tr = stats[3:4]
    h11 = s_all + 1.0
    h22 = s_tr + 1.0
    det = h11 * h22 - s_tr * s_tr
    return (a_coef + (h22 * ga - s_tr * gc) / det, c_coef + (h11 * gc - s_tr * ga) / det)


def kernel(
    n,
    feat_hbm,
    mult_hbm,
    coef_hbm,
    treat_hbm,
    target_hbm,
    offset_hbm,
    low_hbm,
    high_hbm,
    grad_ref,
    hess_ref,
    eff_ref,
    feat,
    mult,
    coef,
    treat_ref,
    target_ref,
    offset_ref,
    low_ref,
    high_ref,
    coef_all,
    wide_weight,
    acc,
    ipw,
    resid,
    curv,
    keep,
    xsend,
    xrecv,
    zsend,
    zrecv,
    sums,
    stat_send,
    stat_recv,
    feat_sem,
    mult_sem,
    coef_sem,
    side_sem,
    ag_up,
    ag_down,
    ag_fwd,
    ag_recv,
    x_send,
    x_recv,
    z_send,
    z_recv,
    st_send,
    st_recv,
):
    outer = n // 2
    rep, width = acc.shape
    cols = coef.shape[0]
    tiles = width // TILE
    me = lax.axis_index("row")
    mo = me // 2
    mx = lax.rem(me, 2)
    px = 1 - mx
    partner = 2 * mo + px

    def block(o, x):
        return 2 * o + x

    low_side = 1 - (2 * mo) // outer
    near = low_side * mo + (1 - low_side) * (outer - 1 - mo)
    far = outer - 1 - near

    def target_of(i):
        j = i - (far - near)
        both = mo + (1 - 2 * lax.rem(j + 2 * outer, 2)) * (near - (j + 2 * outer) // 2 + outer)
        return jnp.where(j < 0, mo + (2 * low_side - 1) * (far - i), both)

    def remote(src, dst, send, recv, row):
        return pltpu.make_async_remote_copy(
            src_ref=src,
            dst_ref=dst,
            send_sem=send,
            recv_sem=recv,
            device_id={"row": row},
            device_id_type=pl.DeviceIdType.MESH,
        )

    def feat_copy(b):
        start = pl.multiple_of(b * cols, cols)
        return pltpu.make_async_copy(feat_hbm.at[:, pl.ds(start, cols)], feat.at[b], feat_sem.at[b])

    coef_copy = pltpu.make_async_copy(coef_hbm, coef, coef_sem)
    coef_copy.start()
    mult_copy = pltpu.make_async_copy(mult_hbm, mult, mult_sem)
    mult_copy.start()
    pairs = (
        (treat_hbm, treat_ref),
        (target_hbm, target_ref),
        (offset_hbm, offset_ref),
        (low_hbm, low_ref),
        (high_hbm, high_ref),
    )
    side_copies = [pltpu.make_async_copy(a, b, side_sem.at[i]) for i, (a, b) in enumerate(pairs)]
    for copy in side_copies:
        copy.start()

    barrier = pltpu.get_barrier_semaphore()
    for j in range(1, n):
        pl.semaphore_signal(
            barrier,
            inc=1,
            device_id={"row": lax.rem(me + j, n)},
            device_id_type=pl.DeviceIdType.MESH,
        )
    coef_copy.wait()
    coef_all[me] = coef[...].astype(F32).T.astype(BF16).reshape(coef_all.shape[1:])
    pl.semaphore_wait(barrier, n - 1)

    def gather_copy(o, h, send, row):
        b = block(o, mx)
        return remote(coef_all.at[b, h], coef_all.at[b, h], send.at[o, h], ag_recv.at[b, h], row)

    def up_copy(o, h):
        return gather_copy(o, h, ag_up, block(mo + 1, mx))

    def down_copy(o, h):
        return gather_copy(o, h, ag_down, block(mo - 1, mx))

    def forward_copy(o, h):
        return gather_copy(o, h, ag_fwd, partner)

    def coef_wait(b, h):
        remote(coef_all.at[b, h], coef_all.at[b, h], ag_fwd.at[0, h], ag_recv.at[b, h], partner).wait_recv()

    has_up = mo + 1 < outer
    has_down = mo > 0

    for h in range(PIECES):
        @pl.when(has_up)
        def _():
            up_copy(mo, h).start()

        @pl.when(has_down)
        def _():
            down_copy(mo, h).start()

        forward_copy(mo, h).start()

    feat_copy(me).start()
    feat_copy(partner).start()

    @pl.loop(1, outer)
    def _(i):
        @pl.when(mo - i >= 0)
        def _():
            feat_copy(block(mo - i, mx)).start()
            feat_copy(block(mo - i, px)).start()

        @pl.when(mo + i < outer)
        def _():
            feat_copy(block(mo + i, mx)).start()
            feat_copy(block(mo + i, px)).start()

    mult_copy.wait()
    for copy in side_copies:
        copy.wait()

    @pl.loop(0, tiles)
    def _(t):
        at = pl.ds(pl.multiple_of(t * TILE, TILE), TILE)
        wide_weight[:, at] = mult[at, :].astype(F32).T

    def logits_of(b, first):
        feat_copy(b).wait()
        part = lax.dot_general(
            coef_all[b].reshape(rep, cols), feat[b], (((1,), (1,)), ((), ())), preferred_element_type=F32
        )
        if first:
            acc[...] = part
        else:
            acc[...] += part

    logits_of(me, True)

    def arrived(b):
        for h in range(PIECES):
            coef_wait(b, h)
        logits_of(b, False)

    @pl.loop(1, outer)
    def _(i):
        below = mo - i
        above = mo + i

        for h in range(PIECES):
            @pl.when(below >= 0)
            def _():
                coef_wait(block(below, mx), h)

                @pl.when(has_up)
                def _():
                    up_copy(below, h).start()

                forward_copy(below, h).start()

            @pl.when(above < outer)
            def _():
                coef_wait(block(above, mx), h)

                @pl.when(has_down)
                def _():
                    down_copy(above, h).start()

                forward_copy(above, h).start()

        @pl.when(below >= 0)
        def _():
            logits_of(block(below, mx), False)

        @pl.when(above < outer)
        def _():
            logits_of(block(above, mx), False)

        @pl.when(below + 1 >= 0)
        def _():
            arrived(block(below + 1, px))

        @pl.when(jnp.logical_and(above - 1 < outer, i > 1))
        def _():
            arrived(block(above - 1, px))

    @pl.when(mo == outer - 1)
    def _():
        arrived(block(0, px))

    @pl.when(mo == 0)
    def _():
        arrived(block(outer - 1, px))

    low = jnp.broadcast_to(low_ref[...].astype(F32) / 256.0, (TILE, rep)).T
    high = jnp.broadcast_to(high_ref[...].astype(F32) / 256.0, (TILE, rep)).T

    def add_sums(weighted, prob, treat, target):
        res = weighted * (target - prob)
        cur = weighted * (prob * (1.0 - prob))
        sums[0] += res
        sums[1] += res * treat
        sums[2] += cur
        sums[3] += cur * treat

    @pl.loop(0, tiles)
    def _(t):
        at = pl.ds(pl.multiple_of(t * TILE, TILE), TILE)
        logit = jnp.minimum(jnp.maximum(acc[:, at], low), high)
        prop = 1.0 / (1.0 + jnp.exp(-logit))
        weight = wide_weight[:, at]
        treat = treat_ref[:, at].astype(F32)
        resid[:, at] = (weight * (treat - prop)).astype(BF16)
        curv[:, at] = (weight * prop * (1.0 - prop)).astype(BF16)

    def first_sums():
        sums[...] = jnp.zeros_like(sums)

        @pl.loop(0, tiles)
        def _(t):
            at = pl.ds(pl.multiple_of(t * TILE, TILE), TILE)
            logit = jnp.minimum(jnp.maximum(acc[:, at], low), high)
            treat = treat_ref[:, at].astype(F32)
            target = target_ref[:, at].astype(F32)
            weighted = wide_weight[:, at] * (1.0 + jnp.exp(jnp.where(treat > 0.5, -logit, logit)))
            ipw[:, at] = weighted
            add_sums(weighted, 1.0 / (1.0 + jnp.exp(-offset_ref[:, at])), treat, target)

    def stat_copy(it, j):
        to = lax.rem(me + j, n)
        return remote(stat_send.at[it], stat_recv.at[it, me], st_send.at[it, j], st_recv.at[it, me], to)

    def send_stats(it):
        for k in range(4):
            stat_send[it, k : k + 1, :] = jnp.sum(sums[k].T, axis=0, keepdims=True)
        stat_send[it, 4:8, :] = jnp.zeros((4, rep), F32)
        stat_recv[it, me] = stat_send[it]
        @pl.loop(1, n)
        def _(j):
            stat_copy(it, j).start()

    def total_stats(it):
        @pl.loop(1, n)
        def _(j):
            src = lax.rem(me + j, n)
            remote(stat_send.at[it], stat_recv.at[it, src], st_send.at[it, j], st_recv.at[it, src], src).wait_recv()
            stat_copy(it, j).wait_send()

        return jnp.sum(stat_recv[it], axis=0)

    def x_copy(o, k):
        return remote(xsend.at[o, k], xrecv.at[o, k], x_send.at[o, k], x_recv.at[o, k], partner)

    def z_direct(o):
        return remote(zsend.at[o, 0], zrecv.at[mo, 0], z_send.at[o, 0], z_recv.at[mo, 0], block(o, mx))

    def z_up(o):
        return remote(zsend.at[o, 1], zrecv.at[o, 1], z_send.at[o, 1], z_recv.at[o, 1], block(mo + 1, mx))

    def z_down(o):
        slot = jnp.where(o == mo - 1, outer, o)
        return remote(zsend.at[o, 1], zrecv.at[slot, 1], z_send.at[o, 1], z_recv.at[slot, 1], block(mo - 1, mx))

    def add_in(o, slot, k):
        remote(zsend.at[0, k], zrecv.at[slot, k], z_send.at[0, k], z_recv.at[slot, k], partner).wait_recv()
        keep[o, k] += zrecv[slot, k].astype(F32)

    def products(b, k):
        if k == 0:
            return jnp.dot(resid[...], feat[b], preferred_element_type=F32)
        wide = feat[b].astype(F32)
        return jnp.dot(curv[...], (wide * wide).astype(BF16), preferred_element_type=F32)

    def compute(o):
        for k in range(2):
            xsend[o, k] = products(block(o, px), k).astype(BF16)
            x_copy(o, k).start()
        for k in range(2):
            keep[o, k] = products(block(o, mx), k)

    def pass_on(o):
        x_copy(o, 0).wait_recv()
        zsend[o, 0] = (keep[o, 0] + xrecv[o, 0].astype(F32)).astype(BF16)
        z_direct(o).start()
        x_copy(o, 1).wait_recv()
        keep[o, 1] += xrecv[o, 1].astype(F32)

        @pl.when(jnp.logical_or(jnp.logical_and(o > mo, has_down), jnp.logical_and(o < mo, has_up)))
        def _():
            add_in(o, o, 1)

        zsend[o, 1] = keep[o, 1].astype(BF16)

        @pl.when(o > mo)
        def _():
            z_up(o).start()

        @pl.when(o < mo)
        def _():
            z_down(o).start()

    compute(target_of(0))
    first_sums()
    send_stats(0)
    compute(target_of(1))

    @pl.loop(2, outer)
    def _(i):
        compute(target_of(i))

        @pl.when(i < outer - 1)
        def _():
            pass_on(target_of(i - 2))

    zero = jnp.zeros((1, rep), F32)
    a_row, c_row = newton_step(zero, zero, total_stats(0))
    a_wide = jnp.broadcast_to(a_row, (TILE, rep)).T
    c_wide = jnp.broadcast_to(c_row, (TILE, rep)).T
    sums[...] = jnp.zeros_like(sums)

    @pl.loop(0, tiles)
    def _(t):
        at = pl.ds(pl.multiple_of(t * TILE, TILE), TILE)
        treat = treat_ref[:, at].astype(F32)
        target = target_ref[:, at].astype(F32)
        offset = offset_ref[:, at]
        prob = 1.0 / (1.0 + jnp.exp(-(a_wide + c_wide * treat + offset)))
        add_sums(ipw[:, at], prob, treat, target)

    send_stats(1)

    for i in range(max(outer - 3, 0), outer - 1):
        pass_on(target_of(i))

    for k in range(2):
        x_copy(mo, k).wait_recv()
        keep[mo, k] += xrecv[mo, k].astype(F32)

    @pl.loop(1, outer)
    def _(i):
        add_in(mo, lax.rem(mo + i, outer), 0)

    @pl.when(has_down)
    def _():
        add_in(mo, mo, 1)

    @pl.when(has_up)
    def _():
        add_in(mo, outer, 1)

    grad_ref[...] = keep[mo, 0].T
    hess_ref[...] = keep[mo, 1].T

    a_row, c_row = newton_step(a_row, c_row, total_stats(1))
    eff_ref[0:1, :] = a_row
    eff_ref[1:2, :] = c_row

    @pl.loop(0, outer)
    def _(o):
        for h in range(PIECES):
            forward_copy(o, h).wait_send()
        for k in range(2):
            x_copy(o, k).wait_send()

        @pl.when(o != mo)
        def _():
            z_direct(o).wait_send()

        @pl.when(has_up)
        def _():
            @pl.when(o <= mo)
            def _():
                for h in range(PIECES):
                    up_copy(o, h).wait_send()

            @pl.when(o > mo)
            def _():
                z_up(o).wait_send()

        @pl.when(has_down)
        def _():
            @pl.when(o >= mo)
            def _():
                for h in range(PIECES):
                    down_copy(o, h).wait_send()

            @pl.when(o < mo)
            def _():
                z_down(o).wait_send()


def local(n, features, coefficients, multiplicity, treated, outcome, offset, trim_low, trim_high):
    rows, depth = features.shape
    cols, rep = coefficients.shape
    outer = n // 2
    hbm = pl.BlockSpec(memory_space=pltpu.HBM)
    vmem = pl.BlockSpec(memory_space=pltpu.VMEM)
    dma = pltpu.SemaphoreType.DMA
    grad, hess, eff = pl.pallas_call(
        functools.partial(kernel, n),
        out_shape=(
            jax.ShapeDtypeStruct((cols, rep), F32),
            jax.ShapeDtypeStruct((cols, rep), F32),
            jax.ShapeDtypeStruct((2, rep), F32),
        ),
        in_specs=[hbm] * 8,
        out_specs=(vmem, vmem, vmem),
        scratch_shapes=[
            pltpu.VMEM((n, rows, cols), BF16),
            pltpu.VMEM((rows, rep), jnp.int32),
            pltpu.VMEM((cols, rep), BF16),
            pltpu.VMEM((1, rows), jnp.int32),
            pltpu.VMEM((1, rows), jnp.int32),
            pltpu.VMEM((1, rows), F32),
            pltpu.VMEM((1, rep), jnp.int32),
            pltpu.VMEM((1, rep), jnp.int32),
            pltpu.VMEM((n, PIECES, rep // PIECES, cols), BF16),
            pltpu.VMEM((rep, rows), F32),
            pltpu.VMEM((rep, rows), F32),
            pltpu.VMEM((rep, rows), F32),
            pltpu.VMEM((rep, rows), BF16),
            pltpu.VMEM((rep, rows), BF16),
            pltpu.VMEM((outer, 2, rep, cols), F32),
            pltpu.VMEM((outer, 2, rep, cols), BF16),
            pltpu.VMEM((outer, 2, rep, cols), BF16),
            pltpu.VMEM((outer, 2, rep, cols), BF16),
            pltpu.VMEM((outer + 1, 2, rep, cols), BF16),
            pltpu.VMEM((4, rep, TILE), F32),
            pltpu.VMEM((REFIT_ITERS, 8, rep), F32),
            pltpu.VMEM((REFIT_ITERS, n, 8, rep), F32),
            dma((n,)),
            dma(()),
            dma(()),
            dma((5,)),
            dma((outer, PIECES)),
            dma((outer, PIECES)),
            dma((outer, PIECES)),
            dma((n, PIECES)),
            dma((outer, 2)),
            dma((outer, 2)),
            dma((outer, 2)),
            dma((outer + 1, 2)),
            dma((REFIT_ITERS, n)),
            dma((REFIT_ITERS, n)),
        ],
        compiler_params=pltpu.CompilerParams(
            collective_id=0, has_side_effects=True, vmem_limit_bytes=63 * 1024 * 1024
        ),
        name="propensity",
    )(
        features,
        multiplicity,
        coefficients,
        treated.reshape(1, rows),
        outcome.reshape(1, rows),
        offset.reshape(1, rows),
        trim_low.reshape(1, rep),
        trim_high.reshape(1, rep),
    )
    hess = hess + 1.0
    new_coefficients = coefficients.astype(F32) + grad / hess
    score = grad / jnp.sqrt(hess)
    owned = rep // n
    mine = lax.dynamic_slice_in_dim(eff, lax.axis_index("row") * owned, owned, axis=1)
    return (new_coefficients, score, mine.reshape(2, 1, owned))


def solution(mesh):
    return jax.shard_map(
        functools.partial(local, mesh.shape["row"]),
        mesh=mesh,
        in_specs=(
            P("row", None),
            P("row", "rep"),
            P("row", "rep"),
            P("row"),
            P("row"),
            P("row"),
            P("rep"),
            P("rep"),
        ),
        out_specs=(P("row", "rep"), P("row", "rep"), P(None, "rep", "row")),
        check_vma=False,
    )
```
